512 devices in a mesh: row: 32 (over y, x), col: 16 (over z, core).
Axes of the slice: x: 4, y: 8, z: 8, core: 2. Of those that a mesh axis runs over, the one named last changes fastest.
Arguments:
- kernel_matrix: float32 [16384, 16384], P('row', 'col'), may hold values from 0 to 2, as said below
Outputs:
- factored: float32 [16384, 16384], P('row', 'col')
The draws below stay inside these ranges and needn't reach their ends.
Inputs may be any that keep to these rules, and one draw needn't show every extreme that they name: kernel_matrix, put in global order by the element-cyclic map, is symmetric: a Gaussian-process kernel amp * exp(-distance / scale) over random points plus a nugget of at least 0.5 on the diagonal, so it is positive definite with smallest eigenvalue at least 0.5.
All inputs are finite; a program needn't handle non-finite values.
Results may differ from the reference program's by a relative error of at most 0.00025.
Values sent between devices are 32-bit elements; how exact they have to be, the bound alone decides.
No kernel may reach another device: no remote copies, remote signals or barrier semaphores. Data moves between devices by JAX's collectives and lax.ppermute only.
A program may use at most 64 MiB of HBM per device.

```python
import jax
import jax.numpy as jnp
from jax import lax

ORDER = 16384
PANEL = 192
PANELS = 2
LOCAL_ROWS = 512
LOCAL_COLS = 1024
N_ROW = 32
N_COL = 16


def draw_kernel_matrix(key, part):
    points = jax.random.uniform(jax.random.fold_in(key, 11), (3, ORDER), jnp.float32)
    length = 0.2
    positions = jnp.arange(ORDER, dtype=jnp.int32)
    row_global = positions % LOCAL_ROWS * (ORDER // LOCAL_ROWS) + positions // LOCAL_ROWS
    col_global = positions % LOCAL_COLS * (ORDER // LOCAL_COLS) + positions // LOCAL_COLS
    row_points = points[:, row_global]
    col_points = points[:, col_global]
    delta_x = row_points[0][:, None] - col_points[0][None, :]
    delta_y = row_points[1][:, None] - col_points[1][None, :]
    delta_z = row_points[2][:, None] - col_points[2][None, :]
    distance = jnp.sqrt(delta_x * delta_x + delta_y * delta_y + delta_z * delta_z)
    kernel = jnp.exp(-distance / length)
    same = (row_global[:, None] == col_global[None, :]).astype(jnp.float32)
    return (kernel + same).astype(jnp.float32)


def setup_inputs(seed: int = 0) -> dict:
    seeds = jax.random.split(jax.random.key(seed), 2)
    kernel_matrix = draw_kernel_matrix(jax.random.fold_in(seeds[1], 71), 0)
    return {"kernel_matrix": kernel_matrix}


def solve_rows(lower_factor, rows):
    return lax.linalg.triangular_solve(lower_factor, rows, left_side=False, lower=True, transpose_a=True)

def reference(kernel_matrix):
    local_rows = ORDER // N_ROW
    local_cols = ORDER // N_COL
    positions = jnp.arange(ORDER)
    row_source = positions % N_ROW * local_rows + positions // N_ROW
    col_source = positions % N_COL * local_cols + positions // N_COL
    global_matrix = kernel_matrix[row_source][:, col_source]
    for current in range(PANELS):
        start = current * PANEL
        corner = global_matrix[start:start + PANEL, start:start + PANEL]
        lower_factor = jnp.linalg.cholesky(corner)
        panel_factor = solve_rows(lower_factor, global_matrix[start:, start:start + PANEL])
        global_matrix = global_matrix.at[start:, start:start + PANEL].set(panel_factor)
        trailing = panel_factor[PANEL:]
        update = jnp.dot(trailing.astype(jnp.float32), trailing.T.astype(jnp.float32), precision=lax.Precision.HIGHEST, preferred_element_type=jnp.float32)
        global_matrix = global_matrix.at[start + PANEL:, start + PANEL:].add(-update)
    row_target = positions % local_rows * N_ROW + positions // local_rows
    col_target = positions % local_cols * N_COL + positions // local_cols
    return global_matrix[row_target][:, col_target]
```

```python
import jax
import jax.numpy as jnp
from jax import lax
from jax.experimental import pallas as pl
from jax.experimental.pallas import tpu as pltpu
from jax.sharding import PartitionSpec as P

PANEL = 192
WIDTH = 384
N_ROW = 32
N_COL = 16
TILE_ROWS = WIDTH // N_ROW
TILE_COLS = WIDTH // N_COL
f32 = jnp.float32


def dot(a, b, over_a, over_b):
    return lax.dot_general(
        a,
        b,
        (((over_a,), (over_b,)), ((), ())),
        precision=lax.Precision.HIGHEST,
        preferred_element_type=f32,
    )


def full(value):
    return jnp.broadcast_to(value, (8, 128))


def factor(block):
    block = list(block)
    count = len(block)
    lane = lax.broadcasted_iota(jnp.int32, (8, 128), 1)
    sub = lax.broadcasted_iota(jnp.int32, (8, 128), 0)
    for q in range(count):
        first = 8 * q
        cols = {
            (i, t): full(block[i][:, first + t : first + t + 1])
            for i in range(q, count)
            for t in range(8)
        }
        e = [[full(cols[q, t][s : s + 1, :]) if s >= t else None for t in range(8)] for s in range(8)]
        scale = [None] * 8
        low = [[None] * 8 for _ in range(8)]
        for t in range(8):
            scale[t] = lax.rsqrt(e[t][t])
            for s in range(t + 1, 8):
                low[s][t] = e[s][t] * scale[t]
            for u in range(t + 1, 8):
                for s in range(u, 8):
                    e[s][u] = e[s][u] - low[s][t] * low[u][t]
        here = (lane >= first) & (lane < first + 8)
        eye = jnp.where(lane - first == sub, 1.0, 0.0).astype(f32)
        own = jnp.where(here, eye, block[q])
        rows = []
        for t in range(8):
            value = full(own[t : t + 1, :])
            for u in range(t):
                value = value - low[t][u] * rows[u]
            rows.append(value * scale[t])
        own = rows[0]
        for t in range(1, 8):
            own = jnp.where(sub == t, rows[t], own)
        block[q] = own
        for i in range(q + 1, count):
            done = []
            total = jnp.where(here, 0.0, block[i])
            for t in range(8):
                value = cols[i, t]
                for u in range(t):
                    value = value - low[t][u] * done[u]
                value = value * scale[t]
                done.append(value)
                total = total - value * rows[t]
            block[i] = total
    return block


def one_hots():
    g = lax.broadcasted_iota(jnp.int32, (WIDTH, WIDTH), 0)
    p = lax.broadcasted_iota(jnp.int32, (WIDTH, WIDTH), 1)
    by_col = jnp.where(p == (g & 15) * TILE_COLS + (g >> 4), 1.0, 0.0).astype(f32)
    by_row = jnp.where(p == (g & 31) * TILE_ROWS + (g >> 5), 1.0, 0.0).astype(f32)
    return by_col, by_row


def factor_kernel(corner_ref, by_row_ref, by_col_ref, s_ref):
    by_col, by_row = one_hots()
    whole = dot(dot(by_col, corner_ref[...], 1, 0), by_row, 1, 1)
    for a in range(3):
        for b in range(3):
            s_ref[a, b] = whole[128 * a : 128 * a + 128, 128 * b : 128 * b + 128]
    row = lax.broadcasted_iota(jnp.int32, (128, 128), 0)
    col = lax.broadcasted_iota(jnp.int32, (128, 128), 1)

    def step(now, _):
        block = factor([s_ref[now, now, 8 * i : 8 * i + 8, :] for i in range(16)])
        inverse = jnp.where(col <= row, jnp.concatenate(block, axis=0), 0.0)
        s_ref[now, now] = inverse
        for b in range(3):

            @pl.when(b != now)
            def _():
                s_ref[now, b] = dot(inverse, s_ref[now, b], 1, 0)

        def update(a, _):
            upper = s_ref[now, a]
            for b in range(3):
                value = dot(upper, s_ref[now, b], 0, 0)

                @pl.when(b != now)
                def _():
                    s_ref[a, b] = s_ref[a, b] - value

                @pl.when(b == now)
                def _():
                    s_ref[a, b] = -value

            return 0

        lax.fori_loop(now + 1, 3, update, 0)
        return 0

    lax.fori_loop(0, 3, step, 0)
    zero = jnp.zeros((128, 128), f32)
    for a in range(3):
        inverse = jnp.concatenate([s_ref[a, b] if b <= a else zero for b in range(3)], axis=1)
        by_row_ref[128 * a : 128 * a + 128, :] = dot(inverse, by_row, 1, 0)
        by_col_ref[128 * a : 128 * a + 128, :] = dot(inverse, by_col, 1, 0)


def update_kernel(col_ref, by_row_ref, by_col_ref, right_ref, left_ref, matrix_ref, out_ref):
    rows = matrix_ref.shape[0]
    left = dot(by_col_ref[...], left_ref[...], 1, 0)
    k = lax.broadcasted_iota(jnp.int32, (WIDTH, 128), 0)
    j = lax.broadcasted_iota(jnp.int32, (WIDTH, 128), 1)
    pick = jnp.where((k == j * N_COL + col_ref[0]) & (j < TILE_COLS), 1.0, 0.0).astype(f32)
    panel = dot(left, pick, 0, 0)
    i = lax.broadcasted_iota(jnp.int32, (WIDTH, rows), 1)
    k = lax.broadcasted_iota(jnp.int32, (WIDTH, rows), 0)
    half = TILE_ROWS // 2
    keep = (i < half) | ((i < TILE_ROWS) & (k >= PANEL))
    left = jnp.where(keep, 0.0, left)
    row = lax.broadcasted_iota(jnp.int32, (rows, 128), 0)
    lane = lax.broadcasted_iota(jnp.int32, (rows, 128), 1)
    in_panel = (lane < TILE_COLS // 2) | ((lane < TILE_COLS) & (row >= half))
    for b in range(4):
        cut = slice(256 * b, 256 * b + 256)
        right = dot(by_row_ref[...], right_ref[:, cut], 1, 0)
        value = matrix_ref[:, cut] - dot(left, right, 0, 0)
        if b == 0:
            out_ref[:, 0:128] = jnp.where(in_panel, panel, value[:, 0:128])
            out_ref[:, 128:256] = value[:, 128:256]
        else:
            out_ref[:, cut] = value


def per_device(matrix):
    local_rows, local_cols = matrix.shape
    top = matrix[:TILE_ROWS]
    right = lax.all_to_all(
        jnp.broadcast_to(top[None], (N_ROW, TILE_ROWS, local_cols)), "row", 0, 0
    ).reshape(WIDTH, local_cols)
    corner = lax.all_gather(right[:, :TILE_COLS].T, "col", axis=0, tiled=True)
    left = lax.all_gather(matrix[:, :TILE_COLS].T, "col", axis=0, tiled=True)
    square = jax.ShapeDtypeStruct((WIDTH, WIDTH), f32)
    by_row, by_col = pl.pallas_call(
        factor_kernel,
        out_shape=(square, square),
        scratch_shapes=[pltpu.VMEM((3, 3, 128, 128), f32)],
    )(corner)
    vmem = pl.BlockSpec(memory_space=pltpu.VMEM)
    return pl.pallas_call(
        update_kernel,
        out_shape=jax.ShapeDtypeStruct((local_rows, local_cols), f32),
        in_specs=[pl.BlockSpec(memory_space=pltpu.SMEM)] + [vmem] * 5,
        out_specs=vmem,
    )(lax.axis_index("col").reshape(1).astype(jnp.int32), by_row, by_col, right, left, matrix)


def solution(mesh):
    return jax.shard_map(
        per_device,
        mesh=mesh,
        in_specs=(P("row", "col"),),
        out_specs=P("row", "col"),
        check_vma=False,
    )
```

```python
import jax
import jax.numpy as jnp
from jax import lax
from jax.experimental import pallas as pl
from jax.experimental.pallas import tpu as pltpu
from jax.sharding import PartitionSpec as P

PANEL = 192
WIDTH = 384
N_ROW = 32
N_COL = 16
TILE_ROWS = WIDTH // N_ROW
TILE_COLS = WIDTH // N_COL
f32 = jnp.float32


def dot(a, b, over_a, over_b):
    return lax.dot_general(
        a,
        b,
        (((over_a,), (over_b,)), ((), ())),
        precision=lax.Precision.HIGHEST,
        preferred_element_type=f32,
    )


def full(value):
    return jnp.broadcast_to(value, (8, 128))


def tree(values):
    values = list(values)
    while len(values) > 1:
        values = [
            values[i] + values[i + 1] if i + 1 < len(values) else values[i]
            for i in range(0, len(values), 2)
        ]
    return values[0]


def factor(block):
    block = list(block)
    count = len(block)
    lane = lax.broadcasted_iota(jnp.int32, (8, 128), 1)
    sub = lax.broadcasted_iota(jnp.int32, (8, 128), 0)
    for q in range(count):
        first = 8 * q
        cols = {
            (i, t): full(block[i][:, first + t : first + t + 1])
            for i in range(q, count)
            for t in range(8)
        }
        e = [[full(cols[q, t][s : s + 1, :]) if s >= t else None for t in range(8)] for s in range(8)]
        scale = [None] * 8
        low = [[None] * 8 for _ in range(8)]
        inv = [[None] * 8 for _ in range(8)]
        for t in range(8):
            scale[t] = lax.rsqrt(e[t][t])
            for s in range(t + 1, 8):
                low[s][t] = e[s][t] * scale[t]
            for u in range(t + 1, 8):
                for s in range(u, 8):
                    e[s][u] = e[s][u] - low[s][t] * low[u][t]
            inv[t][t] = scale[t]
            for u in range(t):
                inv[t][u] = -(tree([low[t][v] * inv[v][u] for v in range(u, t)]) * scale[t])
        here = (lane >= first) & (lane < first + 8)
        eye = jnp.where(lane - first == sub, 1.0, 0.0).astype(f32)
        own = jnp.where(here, eye, block[q])
        raw = [full(own[t : t + 1, :]) for t in range(8)]
        rows = [tree([inv[t][u] * raw[u] for u in range(t + 1)]) for t in range(8)]
        own = rows[0]
        for t in range(1, 8):
            own = jnp.where(sub == t, rows[t], own)
        block[q] = own
        if q + 1 < count:
            back = [tree([inv[u][t] * rows[u] for u in range(t, 8)]) for t in range(8)]
            for i in range(q + 1, count):
                block[i] = jnp.where(here, 0.0, block[i]) - tree(
                    [cols[i, t] * back[t] for t in range(8)]
                )
    return block


def pack_kernel(head_ref, out_ref):
    lane = lax.broadcasted_iota(jnp.int32, (1, 128), 1)
    for a in range(4):
        total = jnp.zeros((1, 128), f32)
        for b in range(4):
            i = 4 * a + b
            if i < TILE_ROWS:
                row = jnp.where(lane < TILE_COLS, head_ref[i : i + 1, :], 0.0)
                total = total + (pltpu.roll(row, 32 * b, 1) if b else row)
        out_ref[:, a, :] = jnp.broadcast_to(total, (N_ROW, 128))


def unpack_kernel(tile_ref, out_ref):
    for a in range(3):
        part = tile_ref[:, a, :]
        stack = jnp.concatenate(
            [part] + [pltpu.roll(part, 128 - 32 * b, 1) for b in range(1, 4)], axis=0
        )
        out_ref[:, 128 * a : 128 * a + 128] = jnp.transpose(stack)[:TILE_COLS]


def factor_kernel(corner_ref, out_ref, s_ref):
    for j in range(TILE_COLS):
        value = corner_ref[:, j, :]
        a, offset = j * N_COL // 128, j * N_COL % 128
        for b in range(a, 3):
            s_ref[a, b, offset : offset + N_COL, :] = value[:, 128 * b : 128 * b + 128]
    row = lax.broadcasted_iota(jnp.int32, (128, 128), 0)
    col = lax.broadcasted_iota(jnp.int32, (128, 128), 1)
    zero = jnp.zeros((128, 128), f32)
    s = {(a, b): s_ref[a, b] for a in range(3) for b in range(a, 3)}
    for p in range(3):
        block = factor([s[p, p][8 * i : 8 * i + 8, :] for i in range(16)])
        own = jnp.where(col <= row, jnp.concatenate(block, axis=0), 0.0)
        w = {b: dot(own, s[p, b], 1, 0) for b in range(3) if b != p}
        w[p] = own
        for b in range(3):
            out_ref[128 * p : 128 * p + 128, 128 * b : 128 * b + 128] = w[b] if b <= p else zero
        for a in range(p + 1, 3):
            for b in [b for b in (1, 2, 0) if b >= a or b <= p]:
                value = dot(w[a], w[b], 0, 0)
                s[a, b] = -value if b == p else s[a, b] - value


def split(value):
    high = value.astype(jnp.bfloat16)
    return high, (value - high.astype(f32)).astype(jnp.bfloat16)


def dot3(a, b, over_a, over_b):
    def one(x, y):
        return lax.dot_general(
            x, y, (((over_a,), (over_b,)), ((), ())), preferred_element_type=f32
        )

    return one(a[0], b[0]) + (one(a[0], b[1]) + one(a[1], b[0]))


def update_kernel(
    col_ref, inv_ref, right_ref, left_ref, matrix_ref, out_ref, rh_ref, rl_ref, lh_ref, ll_ref, panel_ref, ih_ref, il_ref
):
    rows = matrix_ref.shape[0]
    half = TILE_ROWS // 2
    block = pl.program_id(0)

    @pl.when(block == 0)
    def _():
        ih_ref[...], il_ref[...] = split(inv_ref[...])
        for j in range(TILE_COLS):
            cut = slice(N_COL * j, N_COL * j + N_COL)
            lh_ref[cut], ll_ref[cut] = split(left_ref[:, j, :])
        left = dot3((ih_ref[...], il_ref[...]), (lh_ref[...], ll_ref[...]), 1, 0)
        k = lax.broadcasted_iota(jnp.int32, (WIDTH, 128), 0)
        j = lax.broadcasted_iota(jnp.int32, (WIDTH, 128), 1)
        pick = jnp.where((k == j * N_COL + col_ref[0]) & (j < TILE_COLS), 1.0, 0.0).astype(f32)
        panel_ref[...] = dot(left, pick, 0, 0)
        i = lax.broadcasted_iota(jnp.int32, (WIDTH, rows), 1)
        k = lax.broadcasted_iota(jnp.int32, (WIDTH, rows), 0)
        keep = (i < half) | ((i < TILE_ROWS) & (k >= PANEL))
        lh_ref[...], ll_ref[...] = split(jnp.where(keep, 0.0, left))

    for i in range(TILE_ROWS):
        cut = slice(N_ROW * i, N_ROW * i + N_ROW)
        rh_ref[cut], rl_ref[cut] = split(right_ref[:, i, :])
    right = split(dot3((ih_ref[...], il_ref[...]), (rh_ref[...], rl_ref[...]), 1, 0))
    out_ref[...] = matrix_ref[...] - dot3((lh_ref[...], ll_ref[...]), right, 0, 0)

    @pl.when(block == 0)
    def _():
        row = lax.broadcasted_iota(jnp.int32, (rows, 128), 0)
        lane = lax.broadcasted_iota(jnp.int32, (rows, 128), 1)
        in_panel = (lane < TILE_COLS // 2) | ((lane < TILE_COLS) & (row >= half))
        out_ref[:, 0:128] = jnp.where(in_panel, panel_ref[...], out_ref[:, 0:128])


def replicated(value, count):
    return jnp.broadcast_to(value[None], (count,) + value.shape)


def per_device(matrix):
    local_rows, local_cols = matrix.shape
    packed = pl.pallas_call(
        pack_kernel,
        grid=(1,),
        in_specs=[pl.BlockSpec((16, 128), lambda g: (0, 0))],
        out_specs=pl.BlockSpec((N_ROW, 4, 128), lambda g: (0, 0, 0)),
        out_shape=jax.ShapeDtypeStruct((N_ROW, 4, 128), f32),
    )(matrix)
    left = lax.all_gather(matrix[:, :TILE_COLS].T, "col", axis=0)
    packed = lax.all_to_all(packed, "row", 0, 0)
    top = replicated(matrix[:TILE_ROWS], N_ROW)
    packed, left, top = lax.optimization_barrier((packed, left, top))
    right = lax.all_to_all(top, "row", 0, 0)
    tile = pl.pallas_call(
        unpack_kernel, out_shape=jax.ShapeDtypeStruct((TILE_COLS, WIDTH), f32)
    )(packed)
    corner = lax.all_gather(tile, "col", axis=0)
    inverse = pl.pallas_call(
        factor_kernel,
        out_shape=jax.ShapeDtypeStruct((WIDTH, WIDTH), f32),
        scratch_shapes=[pltpu.VMEM((3, 3, 128, 128), f32)],
    )(corner)
    step = 256
    bf16 = jnp.bfloat16
    return pl.pallas_call(
        update_kernel,
        grid=(local_cols // step,),
        out_shape=jax.ShapeDtypeStruct((local_rows, local_cols), f32),
        in_specs=[
            pl.BlockSpec(memory_space=pltpu.SMEM),
            pl.BlockSpec((WIDTH, WIDTH), lambda g: (0, 0)),
            pl.BlockSpec((N_ROW, TILE_ROWS, step), lambda g: (0, 0, g)),
            pl.BlockSpec((N_COL, TILE_COLS, local_rows), lambda g: (0, 0, 0)),
            pl.BlockSpec((local_rows, step), lambda g: (0, g)),
        ],
        out_specs=pl.BlockSpec((local_rows, step), lambda g: (0, g)),
        scratch_shapes=[pltpu.VMEM((WIDTH, step), bf16)] * 2
        + [pltpu.VMEM((WIDTH, local_rows), bf16)] * 2
        + [pltpu.VMEM((local_rows, 128), f32)]
        + [pltpu.VMEM((WIDTH, WIDTH), bf16)] * 2,
    )(lax.axis_index("col").reshape(1).astype(jnp.int32), inverse, right, left, matrix)


def solution(mesh):
    return jax.shard_map(
        per_device,
        mesh=mesh,
        in_specs=(P("row", "col"),),
        out_specs=P("row", "col"),
        check_vma=False,
    )
```

```python
import jax
import jax.numpy as jnp
from jax import lax
from jax.experimental import pallas as pl
from jax.experimental.pallas import tpu as pltpu
from jax.sharding import PartitionSpec as P

PANEL = 192
WIDTH = 384
N_ROW = 32
N_COL = 16
TILE_ROWS = WIDTH // N_ROW
TILE_COLS = WIDTH // N_COL
f32 = jnp.float32


def dot(a, b, over_a, over_b):
    return lax.dot_general(
        a,
        b,
        (((over_a,), (over_b,)), ((), ())),
        precision=lax.Precision.HIGHEST,
        preferred_element_type=f32,
    )


def full(value):
    return jnp.broadcast_to(value, (8, 128))


def tree(values):
    values = list(values)
    while len(values) > 1:
        values = [
            values[i] + values[i + 1] if i + 1 < len(values) else values[i]
            for i in range(0, len(values), 2)
        ]
    return values[0]


def factor(block):
    block = list(block)
    count = len(block)
    lane = lax.broadcasted_iota(jnp.int32, (8, 128), 1)
    sub = lax.broadcasted_iota(jnp.int32, (8, 128), 0)
    for q in range(count):
        first = 8 * q
        cols = {
            (i, t): full(block[i][:, first + t : first + t + 1])
            for i in range(q, count)
            for t in range(8)
        }
        e = [[full(cols[q, t][s : s + 1, :]) if s >= t else None for t in range(8)] for s in range(8)]
        scale = [None] * 8
        low = [[None] * 8 for _ in range(8)]
        inv = [[None] * 8 for _ in range(8)]
        for t in range(8):
            scale[t] = lax.rsqrt(e[t][t])
            for s in range(t + 1, 8):
                low[s][t] = e[s][t] * scale[t]
            for u in range(t + 1, 8):
                for s in range(u, 8):
                    e[s][u] = e[s][u] - low[s][t] * low[u][t]
            inv[t][t] = scale[t]
            for u in range(t):
                inv[t][u] = -(tree([low[t][v] * inv[v][u] for v in range(u, t)]) * scale[t])
        here = (lane >= first) & (lane < first + 8)
        eye = jnp.where(lane - first == sub, 1.0, 0.0).astype(f32)
        own = jnp.where(here, eye, block[q])
        raw = [full(own[t : t + 1, :]) for t in range(8)]
        rows = [tree([inv[t][u] * raw[u] for u in range(t + 1)]) for t in range(8)]
        own = rows[0]
        for t in range(1, 8):
            own = jnp.where(sub == t, rows[t], own)
        block[q] = own
        if q + 1 < count:
            back = [tree([inv[u][t] * rows[u] for u in range(t, 8)]) for t in range(8)]
            for i in range(q + 1, count):
                block[i] = jnp.where(here, 0.0, block[i]) - tree(
                    [cols[i, t] * back[t] for t in range(8)]
                )
    return block


def split(value):
    high = value.astype(jnp.bfloat16)
    return high, (value - high.astype(f32)).astype(jnp.bfloat16)


def dot3(a, b, over_a, over_b):
    def one(x, y):
        return lax.dot_general(
            x, y, (((over_a,), (over_b,)), ((), ())), preferred_element_type=f32
        )

    return one(a[0], b[0]) + (one(a[0], b[1]) + one(a[1], b[0]))


def pack_kernel(head_ref, out_ref):
    lane = lax.broadcasted_iota(jnp.int32, (1, 128), 1)
    for a in range(4):
        total = jnp.zeros((1, 128), f32)
        for b in range(4):
            i = 4 * a + b
            if i < TILE_ROWS:
                row = jnp.where(lane < TILE_COLS, head_ref[i : i + 1, :], 0.0)
                total = total + (pltpu.roll(row, 32 * b, 1) if b else row)
        out_ref[:, a, :] = jnp.broadcast_to(total, (N_ROW, 128))


def unpack_kernel(tile_ref, out_ref):
    for a in range(3):
        part = tile_ref[pl.ds(a, N_ROW, stride=4), :]
        stack = jnp.concatenate(
            [part] + [pltpu.roll(part, 128 - 32 * b, 1) for b in range(1, 4)], axis=0
        )
        out_ref[TILE_COLS * a : TILE_COLS * a + TILE_COLS, :] = jnp.transpose(stack)[:TILE_COLS]


def factor_kernel(corner_ref, high_ref, rest_ref, s_ref):
    for j in range(TILE_COLS):
        a, offset = j * N_COL // 128, j * N_COL % 128
        for b in range(a, 3):
            s_ref[a, b, offset : offset + N_COL, :] = corner_ref[
                pl.ds(TILE_COLS * b + j, N_COL, stride=3 * TILE_COLS), :
            ]
    row = lax.broadcasted_iota(jnp.int32, (128, 128), 0)
    col = lax.broadcasted_iota(jnp.int32, (128, 128), 1)
    zero = jnp.zeros((128, 128), f32)
    s = {(a, b): s_ref[a, b] for a in range(3) for b in range(a, 3)}
    for p in range(3):
        block = factor([s[p, p][8 * i : 8 * i + 8, :] for i in range(16)])
        own = jnp.where(col <= row, jnp.concatenate(block, axis=0), 0.0)
        w = {b: dot(own, s[p, b], 1, 0) for b in range(3) if b != p}
        w[p] = own
        for b in range(3):
            at = (slice(128 * p, 128 * p + 128), slice(128 * b, 128 * b + 128))
            high_ref[at], rest_ref[at] = split(w[b] if b <= p else zero)
        for a in range(p + 1, 3):
            for b in [b for b in (1, 2, 0) if b >= a or b <= p]:
                value = dot(w[a], w[b], 0, 0)
                s[a, b] = -value if b == p else s[a, b] - value


def spread_kernel(head_ref, out_ref):
    chunks = out_ref.shape[1] // TILE_ROWS
    top = jnp.concatenate(
        [head_ref[:TILE_ROWS, 128 * b : 128 * b + 128] for b in range(chunks)], axis=0
    )
    for r in range(N_ROW):
        out_ref[r] = top


def turn_kernel(side_ref, out_ref):
    for b in range(side_ref.shape[0] // 128):
        part = jnp.transpose(side_ref[128 * b : 128 * b + 128, :])
        out_ref[TILE_COLS * b : TILE_COLS * b + TILE_COLS, :] = part[:TILE_COLS]


def left_kernel(col_ref, high_ref, rest_ref, left_ref, qh_ref, ql_ref, panel_ref, s_ref):
    rows = panel_ref.shape[0]
    half = TILE_ROWS // 2
    for j in range(TILE_COLS):
        for b in range(rows // 128):
            s_ref[N_COL * j : N_COL * j + N_COL, 128 * b : 128 * b + 128] = left_ref[
                pl.ds(TILE_COLS * b + j, N_COL, stride=TILE_COLS * rows // 128), :
            ]
    left = split(jnp.transpose(s_ref[...]))
    value = dot3(left, (high_ref[...], rest_ref[...]), 1, 1)
    k = lax.broadcasted_iota(jnp.int32, (WIDTH, 128), 0)
    j = lax.broadcasted_iota(jnp.int32, (WIDTH, 128), 1)
    pick = jnp.where((k == j * N_COL + col_ref[0]) & (j < TILE_COLS), 1.0, 0.0).astype(jnp.bfloat16)
    high, rest = split(value)
    panel_ref[...] = jnp.dot(high, pick, preferred_element_type=f32) + jnp.dot(
        rest, pick, preferred_element_type=f32
    )
    qh_ref[...] = high
    ql_ref[...] = rest
    i = lax.broadcasted_iota(jnp.int32, (16, WIDTH), 0)
    k = lax.broadcasted_iota(jnp.int32, (16, WIDTH), 1)
    keep = (i < half) | ((i < TILE_ROWS) & (k >= PANEL))
    qh_ref[:16, :], ql_ref[:16, :] = split(jnp.where(keep, 0.0, value[:16, :]))


def update_kernel(
    high_ref, rest_ref, qh_ref, ql_ref, panel_ref, right_ref, matrix_ref, out_ref, rh_ref, rl_ref
):
    rows = matrix_ref.shape[0]
    half = TILE_ROWS // 2
    block = pl.program_id(0)
    chunks = rh_ref.shape[1] // 128
    stride = right_ref.shape[0] // N_ROW
    for b in range(chunks):
        lanes = slice(128 * b, 128 * b + 128)
        for i in range(TILE_ROWS):
            cut = slice(N_ROW * i, N_ROW * i + N_ROW)
            first = (block * chunks + b) * TILE_ROWS + i
            rh_ref[cut, lanes], rl_ref[cut, lanes] = split(
                right_ref[pl.ds(first, N_ROW, stride=stride), :]
            )
    right = split(dot3((high_ref[...], rest_ref[...]), (rh_ref[...], rl_ref[...]), 1, 0))
    out_ref[...] = matrix_ref[...] - dot3((qh_ref[...], ql_ref[...]), right, 1, 0)

    @pl.when(block == 0)
    def _():
        row = lax.broadcasted_iota(jnp.int32, (rows, 128), 0)
        lane = lax.broadcasted_iota(jnp.int32, (rows, 128), 1)
        in_panel = (lane < TILE_COLS // 2) | ((lane < TILE_COLS) & (row >= half))
        out_ref[:, 0:128] = jnp.where(in_panel, panel_ref[...], out_ref[:, 0:128])


def finish(col, high, rest, left, right, matrix):
    local_rows, local_cols = matrix.shape
    bf16 = jnp.bfloat16
    vmem = pl.BlockSpec(memory_space=pltpu.VMEM)
    qh, ql, panel = pl.pallas_call(
        left_kernel,
        in_specs=[pl.BlockSpec(memory_space=pltpu.SMEM)] + [vmem] * 3,
        out_shape=(
            jax.ShapeDtypeStruct((local_rows, WIDTH), bf16),
            jax.ShapeDtypeStruct((local_rows, WIDTH), bf16),
            jax.ShapeDtypeStruct((local_rows, 128), f32),
        ),
        scratch_shapes=[pltpu.VMEM((WIDTH, local_rows), f32)],
    )(col, high, rest, left)
    step = 256
    whole = lambda g: (0, 0)
    return pl.pallas_call(
        update_kernel,
        grid=(local_cols // step,),
        out_shape=jax.ShapeDtypeStruct((local_rows, local_cols), f32),
        in_specs=[
            pl.BlockSpec((WIDTH, WIDTH), whole),
            pl.BlockSpec((WIDTH, WIDTH), whole),
            pl.BlockSpec((local_rows, WIDTH), whole),
            pl.BlockSpec((local_rows, WIDTH), whole),
            pl.BlockSpec((local_rows, 128), whole),
            pl.BlockSpec(right.shape, whole),
            pl.BlockSpec((local_rows, step), lambda g: (0, g)),
        ],
        out_specs=pl.BlockSpec((local_rows, step), lambda g: (0, g)),
        scratch_shapes=[pltpu.VMEM((WIDTH, step), bf16)] * 2,
    )(high, rest, qh, ql, panel, right, matrix)


def per_device(matrix):
    local_rows, local_cols = matrix.shape
    packed = pl.pallas_call(
        pack_kernel,
        grid=(1,),
        in_specs=[pl.BlockSpec((16, 128), lambda g: (0, 0))],
        out_specs=pl.BlockSpec((N_ROW, 4, 128), lambda g: (0, 0, 0)),
        out_shape=jax.ShapeDtypeStruct((N_ROW, 4, 128), f32),
    )(matrix)
    packed = lax.all_to_all(packed, "row", 0, 0)
    folded = (N_ROW, TILE_ROWS * local_cols // 128, 128)
    top = pl.pallas_call(
        spread_kernel,
        grid=(1,),
        in_specs=[pl.BlockSpec((16, local_cols), lambda g: (0, 0))],
        out_specs=pl.BlockSpec(folded, lambda g: (0, 0, 0)),
        out_shape=jax.ShapeDtypeStruct(folded, f32),
    )(matrix)
    tall = (TILE_COLS * local_rows // 128, 128)
    turned = pl.pallas_call(
        turn_kernel,
        grid=(1,),
        in_specs=[pl.BlockSpec((local_rows, 128), lambda g: (0, 0))],
        out_specs=pl.BlockSpec(tall, lambda g: (0, 0)),
        out_shape=jax.ShapeDtypeStruct(tall, f32),
    )(matrix)
    packed, top, turned = lax.optimization_barrier((packed, top, turned))
    right = lax.all_to_all(top, "row", 0, 0).reshape(-1, 128)
    tile = pl.pallas_call(
        unpack_kernel, out_shape=jax.ShapeDtypeStruct((3 * TILE_COLS, 128), f32)
    )(packed.reshape(N_ROW * 4, 128))
    corner = lax.all_gather(tile, "col", axis=0, tiled=True)
    corner, turned = lax.optimization_barrier((corner, turned))
    left = lax.all_gather(turned, "col", axis=0, tiled=True)
    square = jax.ShapeDtypeStruct((WIDTH, WIDTH), jnp.bfloat16)
    high, rest = pl.pallas_call(
        factor_kernel,
        out_shape=(square, square),
        scratch_shapes=[pltpu.VMEM((3, 3, 128, 128), f32)],
    )(corner)
    col = lax.axis_index("col").reshape(1).astype(jnp.int32)
    return finish(col, high, rest, left, right, matrix)


def solution(mesh):
    return jax.shard_map(
        per_device,
        mesh=mesh,
        in_specs=(P("row", "col"),),
        out_specs=P("row", "col"),
        check_vma=False,
    )
```

```python
import jax
import jax.numpy as jnp
from jax import lax
from jax.experimental import pallas as pl
from jax.experimental.pallas import tpu as pltpu
from jax.sharding import PartitionSpec as P

PANEL = 192
WIDTH = 384
N_ROW = 32
N_COL = 16
TILE_ROWS = WIDTH // N_ROW
TILE_COLS = WIDTH // N_COL
f32 = jnp.float32


def dot(a, b, over_a, over_b):
    return lax.dot_general(
        a,
        b,
        (((over_a,), (over_b,)), ((), ())),
        precision=lax.Precision.HIGHEST,
        preferred_element_type=f32,
    )


def full(value):
    return jnp.broadcast_to(value, (8, 128))


def tree(values):
    values = list(values)
    while len(values) > 1:
        values = [
            values[i] + values[i + 1] if i + 1 < len(values) else values[i]
            for i in range(0, len(values), 2)
        ]
    return values[0]


def factor(block):
    block = list(block)
    count = len(block)
    lane = lax.broadcasted_iota(jnp.int32, (8, 128), 1)
    sub = lax.broadcasted_iota(jnp.int32, (8, 128), 0)

    def column(i, j):
        return full(block[i][:, j : j + 1])

    diag = [column(0, u) for u in range(8)]
    for q in range(count):
        first = 8 * q
        cols = {(i, t): column(i, first + t) for i in range(q + 1, count) for t in range(8)}
        if q + 1 < count:
            ahead = [column(q + 1, first + 8 + u) for u in range(8)]
        e = [[full(diag[t][s : s + 1, :]) if s >= t else None for t in range(8)] for s in range(8)]
        scale = [None] * 8
        low = [[None] * 8 for _ in range(8)]
        for t in range(8):
            scale[t] = lax.rsqrt(e[t][t])
            for s in range(t + 1, 8):
                low[s][t] = e[s][t] * scale[t]
            for u in range(t + 1, 8):
                for s in range(u, 8):
                    e[s][u] = e[s][u] - low[s][t] * low[u][t]
        here = (lane >= first) & (lane < first + 8)
        eye = jnp.where(lane - first == sub, 1.0, 0.0).astype(f32)
        own = jnp.where(here, eye, block[q])
        if q + 1 < count:
            done = []
            for t in range(8):
                value = cols[q + 1, t]
                for u in range(t):
                    value = value - low[t][u] * done[u]
                done.append(value * scale[t])
            diag = []
            for u in range(8):
                terms = [done[t] * full(done[t][u : u + 1, :]) for t in range(8)]
                diag.append((ahead[u] - tree(terms[:7])) - terms[7])
        rows = []
        for t in range(8):
            value = full(own[t : t + 1, :])
            for u in range(t):
                value = value - low[t][u] * rows[u]
            rows.append(value * scale[t])
        own = rows[0]
        for t in range(1, 8):
            own = jnp.where(sub == t, rows[t], own)
        block[q] = own
        if q + 1 < count:
            back = [None] * 8
            for t in reversed(range(8)):
                value = rows[t]
                for u in range(t + 1, 8):
                    value = value - low[u][t] * back[u]
                back[t] = value * scale[t]
            for i in range(q + 1, count):
                block[i] = jnp.where(here, 0.0, block[i]) - tree(
                    [cols[i, t] * back[t] for t in range(8)]
                )
    return block


def split(value):
    high = value.astype(jnp.bfloat16)
    return high, (value - high.astype(f32)).astype(jnp.bfloat16)


def narrow_dot(a, b, over_a, over_b):
    return lax.dot_general(a, b, (((over_a,), (over_b,)), ((), ())), preferred_element_type=f32)


def put(ref, rows, lanes, value, stacked):
    high, rest = split(value)
    parts = (high, rest, high) if stacked else (high, high, rest)
    for n in range(3):
        if stacked:
            ref[WIDTH * n + rows.start : WIDTH * n + rows.stop, lanes] = parts[n]
        else:
            ref[rows, WIDTH * n + lanes.start : WIDTH * n + lanes.stop] = parts[n]


def pack_kernel(head_ref, out_ref):
    lane = lax.broadcasted_iota(jnp.int32, (1, 128), 1)
    for a in range(4):
        total = jnp.zeros((1, 128), f32)
        for b in range(4):
            i = 4 * a + b
            if i < TILE_ROWS:
                row = jnp.where(lane < TILE_COLS, head_ref[i : i + 1, :], 0.0)
                total = total + (pltpu.roll(row, 32 * b, 1) if b else row)
        out_ref[:, a, :] = jnp.broadcast_to(total, (N_ROW, 128))


def unpack_kernel(tile_ref, out_ref):
    for a in range(3):
        part = tile_ref[pl.ds(a, N_ROW, stride=4), :]
        stack = jnp.concatenate(
            [part] + [pltpu.roll(part, 128 - 32 * b, 1) for b in range(1, 4)], axis=0
        )
        count = 8 * (a + 1)
        out_ref[4 * a * (a + 1) : 4 * a * (a + 1) + count, :] = jnp.transpose(stack)[:count]


def factor_kernel(corner_ref, out_ref, s_ref):
    for j in range(TILE_COLS):
        a, offset = j * N_COL // 128, j * N_COL % 128
        for b in range(a, 3):
            s_ref[a, b, offset : offset + N_COL, :] = corner_ref[
                pl.ds(4 * b * (b + 1) + j, N_COL, stride=2 * TILE_COLS), :
            ]
    row = lax.broadcasted_iota(jnp.int32, (128, 128), 0)
    col = lax.broadcasted_iota(jnp.int32, (128, 128), 1)
    zero = jnp.zeros((128, 128), f32)
    s = {(a, b): s_ref[a, b] for a in range(3) for b in range(a, 3)}
    for p in range(3):
        block = factor([s[p, p][8 * i : 8 * i + 8, :] for i in range(16)])
        own = jnp.where(col <= row, jnp.concatenate(block, axis=0), 0.0)
        w = {b: dot(own, s[p, b], 1, 0) for b in range(3) if b != p}
        w[p] = own
        for b in range(3):
            at = slice(128 * p, 128 * p + 128), slice(128 * b, 128 * b + 128)
            put(out_ref, *at, w[b] if b <= p else zero, False)
        for a in range(p + 1, 3):
            for b in [b for b in (1, 2, 0) if b >= a or b <= p]:
                value = dot(w[a], w[b], 0, 0)
                s[a, b] = -value if b == p else s[a, b] - value


def spread_kernel(head_ref, out_ref):
    chunks = out_ref.shape[1] // TILE_ROWS
    top = jnp.concatenate(
        [head_ref[:TILE_ROWS, 128 * b : 128 * b + 128] for b in range(chunks)], axis=0
    )
    for r in range(N_ROW):
        out_ref[r] = top


def turn_kernel(side_ref, out_ref):
    for b in range(side_ref.shape[0] // 128):
        part = jnp.transpose(side_ref[128 * b : 128 * b + 128, :])
        out_ref[TILE_COLS * b : TILE_COLS * b + TILE_COLS, :] = part[:TILE_COLS]


def left_product(col_ref, inv_ref, left_ref, q_ref, panel_ref, s_ref, t_ref):
    rows = panel_ref.shape[0]
    half = TILE_ROWS // 2
    for j in range(TILE_COLS):
        for b in range(rows // 128):
            s_ref[N_COL * j : N_COL * j + N_COL, 128 * b : 128 * b + 128] = left_ref[
                pl.ds(TILE_COLS * b + j, N_COL, stride=TILE_COLS * rows // 128), :
            ]
    every = slice(0, WIDTH)
    put(t_ref, slice(0, rows), every, jnp.transpose(s_ref[...]), False)
    high = inv_ref[:, 0:WIDTH]
    rest = inv_ref[:, 2 * WIDTH : 3 * WIDTH]
    value = narrow_dot(t_ref[...], jnp.concatenate([high, rest, high], axis=1), 1, 1)
    k = lax.broadcasted_iota(jnp.int32, (WIDTH, 128), 0)
    j = lax.broadcasted_iota(jnp.int32, (WIDTH, 128), 1)
    pick = jnp.where((k == j * N_COL + col_ref[0]) & (j < TILE_COLS), 1.0, 0.0).astype(jnp.bfloat16)
    high, rest = split(value)
    panel_ref[...] = narrow_dot(high, pick, 1, 0) + narrow_dot(rest, pick, 1, 0)
    put(q_ref, slice(0, rows), every, value, False)
    i = lax.broadcasted_iota(jnp.int32, (16, WIDTH), 0)
    k = lax.broadcasted_iota(jnp.int32, (16, WIDTH), 1)
    keep = (i < half) | ((i < TILE_ROWS) & (k >= PANEL))
    put(q_ref, slice(0, 16), every, jnp.where(keep, 0.0, value[:16, :]), False)


def update_kernel(
    col_ref, inv_ref, left_ref, right_ref, matrix_ref, out_ref, r_ref, u_ref, q_ref, panel_ref, s_ref, t_ref
):
    rows = matrix_ref.shape[0]
    half = TILE_ROWS // 2
    block = pl.program_id(0)

    @pl.when(block == 0)
    def _():
        left_product(col_ref, inv_ref, left_ref, q_ref, panel_ref, s_ref, t_ref)

    chunks = r_ref.shape[1] // 128
    stride = right_ref.shape[0] // N_ROW
    for b in range(chunks):
        for i in range(TILE_ROWS):
            first = (block * chunks + b) * TILE_ROWS + i
            put(
                r_ref,
                slice(N_ROW * i, N_ROW * i + N_ROW),
                slice(128 * b, 128 * b + 128),
                right_ref[pl.ds(first, N_ROW, stride=stride), :],
                True,
            )
    value = narrow_dot(inv_ref[...], r_ref[...], 1, 0)
    put(u_ref, slice(0, WIDTH), slice(0, 128 * chunks), value, True)
    out_ref[...] = matrix_ref[...] - narrow_dot(q_ref[...], u_ref[...], 1, 0)

    @pl.when(block == 0)
    def _():
        row = lax.broadcasted_iota(jnp.int32, (rows, 128), 0)
        lane = lax.broadcasted_iota(jnp.int32, (rows, 128), 1)
        in_panel = (lane < TILE_COLS // 2) | ((lane < TILE_COLS) & (row >= half))
        out_ref[:, 0:128] = jnp.where(in_panel, panel_ref[...], out_ref[:, 0:128])


STEP = 512


PARAMS = pltpu.CompilerParams(vmem_limit_bytes=24 << 20)


def near(value):
    return pltpu.with_memory_space_constraint(value, pltpu.VMEM)


def finish(col, inverse, left, right, matrix):
    local_rows, local_cols = matrix.shape
    bf16 = jnp.bfloat16
    vmem = pl.BlockSpec(memory_space=pltpu.VMEM)
    step = STEP
    return pl.pallas_call(
        update_kernel,
        compiler_params=PARAMS,
        grid=(local_cols // step,),
        out_shape=jax.ShapeDtypeStruct((local_rows, local_cols), f32),
        in_specs=[
            pl.BlockSpec(memory_space=pltpu.SMEM),
            vmem,
            vmem,
            vmem,
            pl.BlockSpec((local_rows, step), lambda g: (0, g)),
        ],
        out_specs=pl.BlockSpec((local_rows, step), lambda g: (0, g)),
        scratch_shapes=[pltpu.VMEM((3 * WIDTH, step), bf16)] * 2
        + [
            pltpu.VMEM((local_rows, 3 * WIDTH), bf16),
            pltpu.VMEM((local_rows, 128), f32),
            pltpu.VMEM((WIDTH, local_rows), f32),
            pltpu.VMEM((local_rows, 3 * WIDTH), bf16),
        ],
    )(col, inverse, left, right, matrix)


def per_device(matrix):
    local_rows, local_cols = matrix.shape
    packed = pl.pallas_call(
        pack_kernel,
        grid=(1,),
        in_specs=[pl.BlockSpec((16, 128), lambda g: (0, 0))],
        out_specs=pl.BlockSpec((N_ROW, 4, 128), lambda g: (0, 0, 0)),
        out_shape=jax.ShapeDtypeStruct((N_ROW, 4, 128), f32),
    )(matrix)
    packed = lax.all_to_all(packed, "row", 0, 0)
    folded = (N_ROW, TILE_ROWS * local_cols // 128, 128)
    top = pl.pallas_call(
        spread_kernel,
        grid=(1,),
        in_specs=[pl.BlockSpec((16, local_cols), lambda g: (0, 0))],
        out_specs=pl.BlockSpec(folded, lambda g: (0, 0, 0)),
        out_shape=jax.ShapeDtypeStruct(folded, f32),
    )(matrix)
    tall = (TILE_COLS * local_rows // 128, 128)
    turned = pl.pallas_call(
        turn_kernel,
        grid=(1,),
        in_specs=[pl.BlockSpec((local_rows, 128), lambda g: (0, 0))],
        out_specs=pl.BlockSpec(tall, lambda g: (0, 0)),
        out_shape=jax.ShapeDtypeStruct(tall, f32),
    )(matrix)
    packed, top, turned = lax.optimization_barrier((packed, top, turned))
    right = lax.all_to_all(top, "row", 0, 0).reshape(-1, 128)
    right = near(right)

    tile = pl.pallas_call(
        unpack_kernel,
        compiler_params=PARAMS,
        in_specs=[pl.BlockSpec(memory_space=pltpu.VMEM)],
        out_shape=jax.ShapeDtypeStruct((2 * TILE_COLS, 128), f32),
    )(near(packed.reshape(N_ROW * 4, 128)))
    corner = lax.all_gather(tile, "col", axis=0, tiled=True)
    corner, turned = lax.optimization_barrier((corner, turned))
    left = lax.all_gather(turned, "col", axis=0, tiled=True)
    inverse = pl.pallas_call(
        factor_kernel,
        compiler_params=PARAMS,
        in_specs=[pl.BlockSpec(memory_space=pltpu.VMEM)],
        out_shape=jax.ShapeDtypeStruct((WIDTH, 3 * WIDTH), jnp.bfloat16),
        scratch_shapes=[pltpu.VMEM((3, 3, 128, 128), f32)],
    )(near(corner))
    col = lax.axis_index("col").reshape(1).astype(jnp.int32)
    inverse = near(inverse)
    return finish(col, inverse, left, right, matrix)


def solution(mesh):
    return jax.shard_map(
        per_device,
        mesh=mesh,
        in_specs=(P("row", "col"),),
        out_specs=P("row", "col"),
        check_vma=False,
    )
```

```python
import jax
import jax.numpy as jnp
from jax import lax
from jax.experimental import pallas as pl
from jax.experimental.pallas import tpu as pltpu
from jax.sharding import PartitionSpec as P

PANEL = 192
WIDTH = 384
N_ROW = 32
N_COL = 16
TILE_ROWS = WIDTH // N_ROW
TILE_COLS = WIDTH // N_COL
EARLY = 2
f32 = jnp.float32


def dot(a, b, over_a, over_b):
    return lax.dot_general(
        a,
        b,
        (((over_a,), (over_b,)), ((), ())),
        precision=lax.Precision.HIGHEST,
        preferred_element_type=f32,
    )


def full(value):
    return jnp.broadcast_to(value, (8, 128))


def tree(values):
    values = list(values)
    while len(values) > 1:
        values = [
            values[i] + values[i + 1] if i + 1 < len(values) else values[i]
            for i in range(0, len(values), 2)
        ]
    return values[0]


def factor(block):
    block = list(block)
    count = len(block)
    lane = lax.broadcasted_iota(jnp.int32, (8, 128), 1)
    sub = lax.broadcasted_iota(jnp.int32, (8, 128), 0)

    def column(i, j):
        return full(block[i][:, j : j + 1])

    diag = [column(0, u) for u in range(8)]
    for q in range(count):
        first = 8 * q
        cols = {(i, t): column(i, first + t) for i in range(q + 1, count) for t in range(8)}
        if q + 1 < count:
            ahead = [column(q + 1, first + 8 + u) for u in range(8)]
        e = [[full(diag[t][s : s + 1, :]) if s >= t else None for t in range(8)] for s in range(8)]
        scale = [None] * 8
        low = [[None] * 8 for _ in range(8)]
        for t in range(8):
            scale[t] = lax.rsqrt(e[t][t])
            for s in range(t + 1, 8):
                low[s][t] = e[s][t] * scale[t]
            for u in range(t + 1, 8):
                for s in range(u, 8):
                    e[s][u] = e[s][u] - low[s][t] * low[u][t]
        here = (lane >= first) & (lane < first + 8)
        eye = jnp.where(lane - first == sub, 1.0, 0.0).astype(f32)
        own = jnp.where(here, eye, block[q])
        if q + 1 < count:
            done = []
            for t in range(8):
                value = cols[q + 1, t]
                for u in range(t):
                    value = value - low[t][u] * done[u]
                done.append(value * scale[t])
            diag = []
            for u in range(8):
                terms = [done[t] * full(done[t][u : u + 1, :]) for t in range(8)]
                diag.append((ahead[u] - tree(terms[:7])) - terms[7])
        rows = []
        for t in range(8):
            value = full(own[t : t + 1, :])
            for u in range(t):
                value = value - low[t][u] * rows[u]
            rows.append(value * scale[t])
        own = rows[0]
        for t in range(1, 8):
            own = jnp.where(sub == t, rows[t], own)
        block[q] = own
        if q + 1 < count:
            back = [None] * 8
            for t in reversed(range(8)):
                value = rows[t]
                for u in range(t + 1, 8):
                    value = value - low[u][t] * back[u]
                back[t] = value * scale[t]
            for i in range(q + 1, count):
                block[i] = jnp.where(here, 0.0, block[i]) - tree(
                    [cols[i, t] * back[t] for t in range(8)]
                )
    return block


def split(value):
    high = value.astype(jnp.bfloat16)
    return high, (value - high.astype(f32)).astype(jnp.bfloat16)


def narrow_dot(a, b, over_a, over_b):
    return lax.dot_general(a, b, (((over_a,), (over_b,)), ((), ())), preferred_element_type=f32)


def put(ref, rows, lanes, value, stacked):
    high, rest = split(value)
    parts = (high, rest, high) if stacked else (high, high, rest)
    for n in range(3):
        if stacked:
            ref[WIDTH * n + rows.start : WIDTH * n + rows.stop, lanes] = parts[n]
        else:
            ref[rows, WIDTH * n + lanes.start : WIDTH * n + lanes.stop] = parts[n]


def chunk(ref, b):
    return ref[:TILE_ROWS, 128 * b : 128 * b + 128]


def pack_kernel(head_ref, out_ref):
    top = jnp.concatenate([chunk(head_ref, b) for b in range(EARLY)], axis=0)
    for r in range(N_ROW):
        out_ref[r] = top


def unpack_kernel(tile_ref, out_ref):
    for a in range(3):
        stack = jnp.concatenate(
            [tile_ref[pl.ds(4 * a + b, N_ROW, stride=EARLY * TILE_ROWS), :] for b in range(4)], axis=0
        )
        count = 8 * (a + 1)
        out_ref[4 * a * (a + 1) : 4 * a * (a + 1) + count, :] = jnp.transpose(stack)[:count]


def factor_kernel(corner_ref, out_ref, s_ref):
    for j in range(TILE_COLS):
        a, offset = j * N_COL // 128, j * N_COL % 128
        for b in range(a, 3):
            s_ref[a, b, offset : offset + N_COL, :] = corner_ref[
                pl.ds(4 * b * (b + 1) + j, N_COL, stride=2 * TILE_COLS), :
            ]
    row = lax.broadcasted_iota(jnp.int32, (128, 128), 0)
    col = lax.broadcasted_iota(jnp.int32, (128, 128), 1)
    zero = jnp.zeros((128, 128), f32)
    s = {(a, b): s_ref[a, b] for a in range(3) for b in range(a, 3)}
    for p in range(3):
        block = factor([s[p, p][8 * i : 8 * i + 8, :] for i in range(16)])
        own = jnp.where(col <= row, jnp.concatenate(block, axis=0), 0.0)
        w = {b: dot(own, s[p, b], 1, 0) for b in range(3) if b != p}
        w[p] = own
        for b in range(3):
            at = slice(128 * p, 128 * p + 128), slice(128 * b, 128 * b + 128)
            put(out_ref, *at, w[b] if b <= p else zero, False)
        for a in range(p + 1, 3):
            for b in [b for b in (1, 2, 0) if b >= a or b <= p]:
                value = dot(w[a], w[b], 0, 0)
                s[a, b] = -value if b == p else s[a, b] - value


def spread_kernel(head_ref, side_ref, out_ref, turned_ref):
    chunks = out_ref.shape[1] // TILE_ROWS
    top = jnp.concatenate([chunk(head_ref, EARLY + b) for b in range(chunks)], axis=0)
    for r in range(N_ROW):
        out_ref[r] = top
    for b in range(side_ref.shape[0] // 128):
        part = jnp.transpose(side_ref[128 * b : 128 * b + 128, :])
        turned_ref[TILE_COLS * b : TILE_COLS * b + TILE_COLS, :] = part[:TILE_COLS]


def left_product(col_ref, inv_ref, left_ref, q_ref, panel_ref, s_ref, t_ref):
    rows = panel_ref.shape[0]
    half = TILE_ROWS // 2
    for j in range(TILE_COLS):
        for b in range(rows // 128):
            s_ref[N_COL * j : N_COL * j + N_COL, 128 * b : 128 * b + 128] = left_ref[
                pl.ds(TILE_COLS * b + j, N_COL, stride=TILE_COLS * rows // 128), :
            ]
    every = slice(0, WIDTH)
    put(t_ref, slice(0, rows), every, jnp.transpose(s_ref[...]), False)
    high = inv_ref[:, 0:WIDTH]
    rest = inv_ref[:, 2 * WIDTH : 3 * WIDTH]
    value = narrow_dot(t_ref[...], jnp.concatenate([high, rest, high], axis=1), 1, 1)
    k = lax.broadcasted_iota(jnp.int32, (WIDTH, 128), 0)
    j = lax.broadcasted_iota(jnp.int32, (WIDTH, 128), 1)
    pick = jnp.where((k == j * N_COL + col_ref[0]) & (j < TILE_COLS), 1.0, 0.0).astype(jnp.bfloat16)
    high, rest = split(value)
    panel_ref[...] = narrow_dot(high, pick, 1, 0) + narrow_dot(rest, pick, 1, 0)
    put(q_ref, slice(0, rows), every, value, False)
    i = lax.broadcasted_iota(jnp.int32, (16, WIDTH), 0)
    k = lax.broadcasted_iota(jnp.int32, (16, WIDTH), 1)
    keep = (i < half) | ((i < TILE_ROWS) & (k >= PANEL))
    put(q_ref, slice(0, 16), every, jnp.where(keep, 0.0, value[:16, :]), False)


def update_kernel(
    col_ref, inv_ref, left_ref, early_ref, right_ref, matrix_ref, out_ref, r_ref, u_ref, q_ref, panel_ref, s_ref, t_ref
):
    rows = matrix_ref.shape[0]
    half = TILE_ROWS // 2
    block = pl.program_id(0)

    @pl.when(block == 0)
    def _():
        left_product(col_ref, inv_ref, left_ref, q_ref, panel_ref, s_ref, t_ref)

    chunks = r_ref.shape[1] // 128

    def fetch(ref, b, number):
        for i in range(TILE_ROWS):
            put(
                r_ref,
                slice(N_ROW * i, N_ROW * i + N_ROW),
                slice(128 * b, 128 * b + 128),
                ref[pl.ds(number * TILE_ROWS + i, N_ROW, stride=ref.shape[0] // N_ROW), :],
                True,
            )

    for b in range(chunks):
        if b < EARLY:

            @pl.when(block == 0)
            def _():
                fetch(early_ref, b, b)

            @pl.when(block != 0)
            def _():
                fetch(right_ref, b, block * chunks + b - EARLY)
        else:
            fetch(right_ref, b, block * chunks + b - EARLY)
    value = narrow_dot(inv_ref[...], r_ref[...], 1, 0)
    put(u_ref, slice(0, WIDTH), slice(0, 128 * chunks), value, True)
    out_ref[...] = matrix_ref[...] - narrow_dot(q_ref[...], u_ref[...], 1, 0)

    @pl.when(block == 0)
    def _():
        row = lax.broadcasted_iota(jnp.int32, (rows, 128), 0)
        lane = lax.broadcasted_iota(jnp.int32, (rows, 128), 1)
        in_panel = (lane < TILE_COLS // 2) | ((lane < TILE_COLS) & (row >= half))
        out_ref[:, 0:128] = jnp.where(in_panel, panel_ref[...], out_ref[:, 0:128])


STEP = 512


PARAMS = pltpu.CompilerParams(vmem_limit_bytes=24 << 20)


def near(value):
    return pltpu.with_memory_space_constraint(value, pltpu.VMEM)


def finish(col, inverse, left, early, right, matrix):
    local_rows, local_cols = matrix.shape
    bf16 = jnp.bfloat16
    vmem = pl.BlockSpec(memory_space=pltpu.VMEM)
    step = STEP
    return pl.pallas_call(
        update_kernel,
        grid=(local_cols // step,),
        out_shape=jax.ShapeDtypeStruct((local_rows, local_cols), f32),
        in_specs=[
            pl.BlockSpec(memory_space=pltpu.SMEM),
            vmem,
            vmem,
            vmem,
            vmem,
            pl.BlockSpec((local_rows, step), lambda g: (0, g)),
        ],
        out_specs=pl.BlockSpec((local_rows, step), lambda g: (0, g)),
        scratch_shapes=[pltpu.VMEM((3 * WIDTH, step), bf16)] * 2
        + [
            pltpu.VMEM((local_rows, 3 * WIDTH), bf16),
            pltpu.VMEM((local_rows, 128), f32),
            pltpu.VMEM((WIDTH, local_rows), f32),
            pltpu.VMEM((local_rows, 3 * WIDTH), bf16),
        ],
    )(col, inverse, left, early, right, matrix)


def per_device(matrix):
    local_rows, local_cols = matrix.shape
    chunks = local_cols // 128
    first = (N_ROW, TILE_ROWS * EARLY, 128)
    early = pl.pallas_call(
        pack_kernel,
        grid=(1,),
        in_specs=[pl.BlockSpec((16, 128 * EARLY), lambda g: (0, 0))],
        out_specs=pl.BlockSpec(first, lambda g: (0, 0, 0)),
        out_shape=jax.ShapeDtypeStruct(first, f32),
    )(matrix)
    early = lax.all_to_all(early, "row", 0, 0)
    late = (N_ROW, TILE_ROWS * (chunks - EARLY), 128)
    tall = (TILE_COLS * local_rows // 128, 128)
    top, turned = pl.pallas_call(
        spread_kernel,
        grid=(1,),
        in_specs=[
            pl.BlockSpec((16, local_cols), lambda g: (0, 0)),
            pl.BlockSpec((local_rows, 128), lambda g: (0, 0)),
        ],
        out_specs=(
            pl.BlockSpec(late, lambda g: (0, 0, 0)),
            pl.BlockSpec(tall, lambda g: (0, 0)),
        ),
        out_shape=(jax.ShapeDtypeStruct(late, f32), jax.ShapeDtypeStruct(tall, f32)),
    )(matrix, matrix)
    left = lax.all_gather(turned, "col", axis=0, tiled=True)
    early, top, left = lax.optimization_barrier((early, top, left))
    right = near(lax.all_to_all(top, "row", 0, 0).reshape(-1, 128))
    early = near(early.reshape(-1, 128))
    tile = pl.pallas_call(
        unpack_kernel,
        compiler_params=PARAMS,
        in_specs=[pl.BlockSpec(memory_space=pltpu.VMEM)],
        out_shape=jax.ShapeDtypeStruct((2 * TILE_COLS, 128), f32),
    )(early)
    corner = near(lax.all_gather(near(tile), "col", axis=0, tiled=True))
    inverse = pl.pallas_call(
        factor_kernel,
        in_specs=[pl.BlockSpec(memory_space=pltpu.VMEM)],
        out_shape=jax.ShapeDtypeStruct((WIDTH, 3 * WIDTH), jnp.bfloat16),
        scratch_shapes=[pltpu.VMEM((3, 3, 128, 128), f32)],
    )(corner)

    col = lax.axis_index("col").reshape(1).astype(jnp.int32)
    return finish(col, inverse, left, early, right, matrix)


def solution(mesh):
    return jax.shard_map(
        per_device,
        mesh=mesh,
        in_specs=(P("row", "col"),),
        out_specs=P("row", "col"),
        check_vma=False,
    )
```

```python
import jax
import jax.numpy as jnp
from jax import lax
from jax.experimental import pallas as pl
from jax.experimental.pallas import tpu as pltpu
from jax.sharding import PartitionSpec as P

PANEL = 192
WIDTH = 384
N_ROW = 32
N_COL = 16
TILE_ROWS = WIDTH // N_ROW
TILE_COLS = WIDTH // N_COL
EARLY = 4
f32 = jnp.float32


def dot(a, b, over_a, over_b):
    return lax.dot_general(
        a,
        b,
        (((over_a,), (over_b,)), ((), ())),
        precision=lax.Precision.HIGHEST,
        preferred_element_type=f32,
    )


def full(value):
    return jnp.broadcast_to(value, (8, 128))


def tree(values):
    values = list(values)
    while len(values) > 1:
        values = [
            values[i] + values[i + 1] if i + 1 < len(values) else values[i]
            for i in range(0, len(values), 2)
        ]
    return values[0]


def factor(block):
    block = list(block)
    count = len(block)
    lane = lax.broadcasted_iota(jnp.int32, (8, 128), 1)
    sub = lax.broadcasted_iota(jnp.int32, (8, 128), 0)

    def column(i, j):
        return full(block[i][:, j : j + 1])

    diag = [column(0, u) for u in range(8)]
    for q in range(count):
        first = 8 * q
        cols = {(i, t): column(i, first + t) for i in range(q + 1, count) for t in range(8)}
        if q + 1 < count:
            ahead = [column(q + 1, first + 8 + u) for u in range(8)]
        e = [[full(diag[t][s : s + 1, :]) if s >= t else None for t in range(8)] for s in range(8)]
        scale = [None] * 8
        low = [[None] * 8 for _ in range(8)]
        for t in range(8):
            scale[t] = lax.rsqrt(e[t][t])
            for s in range(t + 1, 8):
                low[s][t] = e[s][t] * scale[t]
            for u in range(t + 1, 8):
                for s in range(u, 8):
                    e[s][u] = e[s][u] - low[s][t] * low[u][t]
        here = (lane >= first) & (lane < first + 8)
        eye = jnp.where(lane - first == sub, 1.0, 0.0).astype(f32)
        own = jnp.where(here, eye, block[q])
        if q + 1 < count:
            done = []
            for t in range(8):
                value = cols[q + 1, t]
                for u in range(t):
                    value = value - low[t][u] * done[u]
                done.append(value * scale[t])
            diag = []
            for u in range(8):
                terms = [done[t] * full(done[t][u : u + 1, :]) for t in range(8)]
                diag.append((ahead[u] - tree(terms[:7])) - terms[7])
        rows = []
        for t in range(8):
            value = full(own[t : t + 1, :])
            for u in range(t):
                value = value - low[t][u] * rows[u]
            rows.append(value * scale[t])
        own = rows[0]
        for t in range(1, 8):
            own = jnp.where(sub == t, rows[t], own)
        block[q] = own
        if q + 1 < count:
            back = [None] * 8
            for t in reversed(range(8)):
                value = rows[t]
                for u in range(t + 1, 8):
                    value = value - low[u][t] * back[u]
                back[t] = value * scale[t]
            for i in range(q + 1, count):
                block[i] = jnp.where(here, 0.0, block[i]) - tree(
                    [cols[i, t] * back[t] for t in range(8)]
                )
    return block


def split(value):
    high = value.astype(jnp.bfloat16)
    return high, (value - high.astype(f32)).astype(jnp.bfloat16)


def narrow_dot(a, b, over_a, over_b):
    return lax.dot_general(a, b, (((over_a,), (over_b,)), ((), ())), preferred_element_type=f32)


def put(ref, rows, lanes, value, stacked):
    high, rest = split(value)
    parts = (high, rest, high) if stacked else (high, high, rest)
    for n in range(3):
        if stacked:
            ref[WIDTH * n + rows.start : WIDTH * n + rows.stop, lanes] = parts[n]
        else:
            ref[rows, WIDTH * n + lanes.start : WIDTH * n + lanes.stop] = parts[n]


def chunk(ref, b):
    return ref[:TILE_ROWS, 128 * b : 128 * b + 128]


def pack_kernel(head_ref, out_ref):
    top = jnp.concatenate([chunk(head_ref, b) for b in range(EARLY)], axis=0)
    for r in range(N_ROW):
        out_ref[r] = top


def unpack_kernel(tile_ref, out_ref):
    for a in range(3):
        stack = jnp.concatenate(
            [tile_ref[pl.ds(4 * a + b, N_ROW, stride=EARLY * TILE_ROWS), :] for b in range(4)], axis=0
        )
        count = 8 * (a + 1)
        out_ref[4 * a * (a + 1) : 4 * a * (a + 1) + count, :] = jnp.transpose(stack)[:count]


def factor_kernel(corner_ref, out_ref, s_ref):
    for j in range(TILE_COLS):
        a, offset = j * N_COL // 128, j * N_COL % 128
        for b in range(a, 3):
            s_ref[a, b, offset : offset + N_COL, :] = corner_ref[
                pl.ds(4 * b * (b + 1) + j, N_COL, stride=2 * TILE_COLS), :
            ]
    row = lax.broadcasted_iota(jnp.int32, (128, 128), 0)
    col = lax.broadcasted_iota(jnp.int32, (128, 128), 1)
    zero = jnp.zeros((128, 128), f32)
    s = {(a, b): s_ref[a, b] for a in range(3) for b in range(a, 3)}
    for p in range(3):
        block = factor([s[p, p][8 * i : 8 * i + 8, :] for i in range(16)])
        own = jnp.where(col <= row, jnp.concatenate(block, axis=0), 0.0)
        w = {b: dot(own, s[p, b], 1, 0) for b in range(3) if b != p}
        w[p] = own
        for b in range(3):
            at = slice(128 * p, 128 * p + 128), slice(128 * b, 128 * b + 128)
            put(out_ref, *at, w[b] if b <= p else zero, False)
        for a in range(p + 1, 3):
            for b in [b for b in (1, 2, 0) if b >= a or b <= p]:
                value = dot(w[a], w[b], 0, 0)
                s[a, b] = -value if b == p else s[a, b] - value


def spread_kernel(head_ref, side_ref, out_ref, turned_ref):
    chunks = out_ref.shape[1] // TILE_ROWS
    top = jnp.concatenate([chunk(head_ref, EARLY + b) for b in range(chunks)], axis=0)
    for r in range(N_ROW):
        out_ref[r] = top
    for b in range(side_ref.shape[0] // 128):
        part = jnp.transpose(side_ref[128 * b : 128 * b + 128, :])
        turned_ref[TILE_COLS * b : TILE_COLS * b + TILE_COLS, :] = part[:TILE_COLS]


def left_product(col_ref, inv_ref, left_ref, q_ref, panel_ref, s_ref, t_ref):
    rows = panel_ref.shape[0]
    half = TILE_ROWS // 2
    for j in range(TILE_COLS):
        for b in range(rows // 128):
            s_ref[N_COL * j : N_COL * j + N_COL, 128 * b : 128 * b + 128] = left_ref[
                pl.ds(TILE_COLS * b + j, N_COL, stride=TILE_COLS * rows // 128), :
            ]
    every = slice(0, WIDTH)
    put(t_ref, slice(0, rows), every, jnp.transpose(s_ref[...]), False)
    high = inv_ref[:, 0:WIDTH]
    rest = inv_ref[:, 2 * WIDTH : 3 * WIDTH]
    value = narrow_dot(t_ref[...], jnp.concatenate([high, rest, high], axis=1), 1, 1)
    k = lax.broadcasted_iota(jnp.int32, (WIDTH, 128), 0)
    j = lax.broadcasted_iota(jnp.int32, (WIDTH, 128), 1)
    pick = jnp.where((k == j * N_COL + col_ref[0]) & (j < TILE_COLS), 1.0, 0.0).astype(jnp.bfloat16)
    high, rest = split(value)
    panel_ref[...] = narrow_dot(high, pick, 1, 0) + narrow_dot(rest, pick, 1, 0)
    put(q_ref, slice(0, rows), every, value, False)
    i = lax.broadcasted_iota(jnp.int32, (16, WIDTH), 0)
    k = lax.broadcasted_iota(jnp.int32, (16, WIDTH), 1)
    keep = (i < half) | ((i < TILE_ROWS) & (k >= PANEL))
    put(q_ref, slice(0, 16), every, jnp.where(keep, 0.0, value[:16, :]), False)


def update_kernel(
    col_ref, inv_ref, left_ref, early_ref, right_ref, matrix_ref, out_ref, r_ref, u_ref, q_ref, panel_ref, s_ref, t_ref
):
    rows = matrix_ref.shape[0]
    half = TILE_ROWS // 2
    block = pl.program_id(0)

    @pl.when(block == 0)
    def _():
        left_product(col_ref, inv_ref, left_ref, q_ref, panel_ref, s_ref, t_ref)

    chunks = r_ref.shape[1] // 128

    def fetch(ref, b, number):
        for i in range(TILE_ROWS):
            put(
                r_ref,
                slice(N_ROW * i, N_ROW * i + N_ROW),
                slice(128 * b, 128 * b + 128),
                ref[pl.ds(number * TILE_ROWS + i, N_ROW, stride=ref.shape[0] // N_ROW), :],
                True,
            )

    for b in range(chunks):
        if b < EARLY:

            @pl.when(block == 0)
            def _():
                fetch(early_ref, b, b)

            @pl.when(block != 0)
            def _():
                fetch(right_ref, b, block * chunks + b - EARLY)
        else:
            fetch(right_ref, b, block * chunks + b - EARLY)
    value = narrow_dot(inv_ref[...], r_ref[...], 1, 0)
    put(u_ref, slice(0, WIDTH), slice(0, 128 * chunks), value, True)
    out_ref[...] = matrix_ref[...] - narrow_dot(q_ref[...], u_ref[...], 1, 0)

    @pl.when(block == 0)
    def _():
        row = lax.broadcasted_iota(jnp.int32, (rows, 128), 0)
        lane = lax.broadcasted_iota(jnp.int32, (rows, 128), 1)
        in_panel = (lane < TILE_COLS // 2) | ((lane < TILE_COLS) & (row >= half))
        out_ref[:, 0:128] = jnp.where(in_panel, panel_ref[...], out_ref[:, 0:128])


STEP = 512


PARAMS = pltpu.CompilerParams(vmem_limit_bytes=24 << 20)


def near(value):
    return pltpu.with_memory_space_constraint(value, pltpu.VMEM)


def finish(col, inverse, left, early, right, matrix):
    local_rows, local_cols = matrix.shape
    bf16 = jnp.bfloat16
    vmem = pl.BlockSpec(memory_space=pltpu.VMEM)
    step = STEP
    return pl.pallas_call(
        update_kernel,
        grid=(local_cols // step,),
        out_shape=jax.ShapeDtypeStruct((local_rows, local_cols), f32),
        in_specs=[
            pl.BlockSpec(memory_space=pltpu.SMEM),
            vmem,
            vmem,
            vmem,
            vmem,
            pl.BlockSpec((local_rows, step), lambda g: (0, g)),
        ],
        out_specs=pl.BlockSpec((local_rows, step), lambda g: (0, g)),
        scratch_shapes=[pltpu.VMEM((3 * WIDTH, step), bf16)] * 2
        + [
            pltpu.VMEM((local_rows, 3 * WIDTH), bf16),
            pltpu.VMEM((local_rows, 128), f32),
            pltpu.VMEM((WIDTH, local_rows), f32),
            pltpu.VMEM((local_rows, 3 * WIDTH), bf16),
        ],
    )(col, inverse, left, early, right, matrix)


def per_device(matrix):
    local_rows, local_cols = matrix.shape
    chunks = local_cols // 128
    first = (N_ROW, TILE_ROWS * EARLY, 128)
    early = pl.pallas_call(
        pack_kernel,
        grid=(1,),
        in_specs=[pl.BlockSpec((16, 128 * EARLY), lambda g: (0, 0))],
        out_specs=pl.BlockSpec(first, lambda g: (0, 0, 0)),
        out_shape=jax.ShapeDtypeStruct(first, f32),
    )(matrix)
    early = lax.all_to_all(early, "row", 0, 0)
    late = (N_ROW, TILE_ROWS * (chunks - EARLY), 128)
    tall = (TILE_COLS * local_rows // 128, 128)
    top, turned = pl.pallas_call(
        spread_kernel,
        grid=(1,),
        in_specs=[
            pl.BlockSpec((16, local_cols), lambda g: (0, 0)),
            pl.BlockSpec((local_rows, 128), lambda g: (0, 0)),
        ],
        out_specs=(
            pl.BlockSpec(late, lambda g: (0, 0, 0)),
            pl.BlockSpec(tall, lambda g: (0, 0)),
        ),
        out_shape=(jax.ShapeDtypeStruct(late, f32), jax.ShapeDtypeStruct(tall, f32)),
    )(matrix, matrix)
    left = lax.all_gather(turned, "col", axis=0, tiled=True)
    early, top, left = lax.optimization_barrier((early, top, left))
    right = near(lax.all_to_all(top, "row", 0, 0).reshape(-1, 128))
    early = near(early.reshape(-1, 128))
    tile = pl.pallas_call(
        unpack_kernel,
        compiler_params=PARAMS,
        in_specs=[pl.BlockSpec(memory_space=pltpu.VMEM)],
        out_shape=jax.ShapeDtypeStruct((2 * TILE_COLS, 128), f32),
    )(early)
    corner = near(lax.all_gather(near(tile), "col", axis=0, tiled=True))
    inverse = pl.pallas_call(
        factor_kernel,
        in_specs=[pl.BlockSpec(memory_space=pltpu.VMEM)],
        out_shape=jax.ShapeDtypeStruct((WIDTH, 3 * WIDTH), jnp.bfloat16),
        scratch_shapes=[pltpu.VMEM((3, 3, 128, 128), f32)],
    )(corner)

    col = lax.axis_index("col").reshape(1).astype(jnp.int32)
    return finish(col, inverse, left, early, right, matrix)


def solution(mesh):
    return jax.shard_map(
        per_device,
        mesh=mesh,
        in_specs=(P("row", "col"),),
        out_specs=P("row", "col"),
        check_vma=False,
    )
```
